128 devices in a mesh: blk: 8 (over x, y_hi), sub: 2 (over y_lo), feat: 8 (over z, core).
Axes of the slice: x: 4, y: 4 (y_hi: 2, y_lo: 2; y = y_hi * 2 + y_lo), z: 4, core: 2. Of those that a mesh axis runs over, the one named last changes fastest.
Arguments:
- sources: bfloat16 [131072, 1024], P(('blk', 'sub'), 'feat'), may hold values from -6 to 6
- adjacency: bfloat16 [16, 16, 32, 128, 128], P(('blk', 'sub')), may hold values from -0.15625 to 0.15625
- target_block: int32 [16, 16, 32], P(('blk', 'sub')), may hold values from 0 to 7
- source_block: int32 [16, 16, 32], P(('blk', 'sub')), may hold values from 0 to 63
- slot_counts: int32 [16, 16], P(('blk', 'sub')), may hold values from 1 to 32, as said below
- weight: bfloat16 [1024, 1024], P(None, 'feat'), may hold values from -0.1875 to 0.1875
Outputs:
- activated: bfloat16 [16384, 1024], P(('blk', 'sub'), 'feat')
The draws below stay inside these ranges and needn't reach their ends.
Inputs may be any that keep to these rules, and one draw needn't show every extreme that they name: Every stripe and piece uses its first slot_counts slots; in every draw some stripe and piece uses all 32.
All inputs are finite; a program needn't handle non-finite values.
Results may differ from the reference program's by a relative error of at most 0.0049.
Values may be sent and summed in bfloat16 or wider, within the bound.
A program may use at most 192 MiB of HBM per device.

```python
import jax
import jax.numpy as jnp
from jax import lax

F = 1024
BLOCK = 128
TGT_DEV = 1024
SRC_DEV = 8192
NSTRIPE = 16
SLOTS = 32
TGT = 16384
SRC = 131072


def draw_slot_counts(key, part):
    key_level = jax.random.fold_in(key, 11)
    key_count = jax.random.fold_in(key, 12)
    key_pick = jax.random.fold_in(key, 13)
    level = jnp.left_shift(jnp.int32(1), jax.random.randint(key_level, (NSTRIPE, 1), 0, 4))
    ceiling = jnp.maximum(1, SLOTS * level // 8)
    lowest = (ceiling + 1) // 2
    spread = jax.random.randint(key_count, (NSTRIPE, NSTRIPE), 0, 1 << 20)
    counts = lowest + spread % (ceiling - lowest + 1)
    picked = jax.random.randint(key_pick, (), 0, NSTRIPE * NSTRIPE)
    flat_counts = counts.reshape(-1).at[picked].set(SLOTS)
    return flat_counts.reshape(NSTRIPE, NSTRIPE).astype(jnp.int32)


def plant(result, stream_key, least, high):
    longest = result.shape.index(max(result.shape))
    spots = []
    for shift in (0, 1):
        where = [jax.random.randint(jax.random.fold_in(stream_key, axis), (), 0, length) for axis, length in enumerate(result.shape)]
        where[longest] = (where[longest] + shift) % result.shape[longest]
        spots.append(tuple(where))
    return result.at[spots[0]].set(least).at[spots[1]].set(high)


def spiked(entries, key, source, target, shards_of, factor):
    def block_of(dim):
        return (jnp.arange(entries.shape[dim]) // (entries.shape[dim] // shards_of)).reshape((-1,) + (1,) * (entries.ndim - 1 - dim))

    near = jax.random.permutation(key, shards_of)[block_of(target)]
    second = (block_of(target) + shards_of // 2) % shards_of
    return jnp.where((block_of(source) == near) | (block_of(source) == second), factor * entries, entries)


def levels(rng, dims, cuts, smallest, top_value):
    gain, own = 1.0, jax.random.fold_in(rng, 6)
    for dim, blocks in cuts:
        heights = jnp.exp(jax.random.uniform(jax.random.fold_in(own, dim), (blocks,), jnp.float32, smallest / len(cuts), top_value / len(cuts)))
        gain = gain * jnp.repeat(heights, dims[dim] // blocks).reshape([-1 if axis == dim else 1 for axis in range(len(dims))])
    return gain


def normal_values(own_key, extent, scale, reach, pieces=(), kind=jnp.bfloat16):
    values = scale * jax.random.normal(own_key, extent, jnp.float32)
    if pieces:
        values = values * levels(own_key, extent, pieces, -0.22, 0.18)
    return jnp.clip(values, -reach, reach).astype(kind)


def bell_draw_with(own_key, shape, scale, most, shards, heavy, kind=jnp.bfloat16):
    values = scale * jax.random.normal(own_key, shape, jnp.float32)
    if shards:
        values = values * levels(own_key, shape, shards, -0.22, 0.18)
    return jnp.clip(spiked(values, jax.random.fold_in(own_key, 3), *heavy), -most, most).astype(kind)


def setup_inputs(seed: int = 0) -> dict:
    key_list = jax.random.split(jax.random.key(seed), 7)
    sources = normal_values(key_list[0], (SRC, F), 1.0, 6.0, ((0, 16), (1, 8)))
    adjacency = bell_draw_with(key_list[1], (NSTRIPE, NSTRIPE, SLOTS, BLOCK, BLOCK), (NSTRIPE * SLOTS * BLOCK * BLOCK // (3 * TGT_DEV)) ** -0.5, 0.15625, ((0, 16),), (0, 1, 16, 2.0))
    target_block = plant(jax.random.randint(key_list[2], (NSTRIPE, NSTRIPE, SLOTS), 0, TGT_DEV // BLOCK), jax.random.fold_in(key_list[2], 1), 0, (TGT_DEV // BLOCK) - 1).astype(jnp.int32)
    source_block = plant(jax.random.randint(key_list[3], (NSTRIPE, NSTRIPE, SLOTS), 0, SRC_DEV // BLOCK), jax.random.fold_in(key_list[3], 1), 0, (SRC_DEV // BLOCK) - 1).astype(jnp.int32)
    slot_counts = draw_slot_counts(jax.random.fold_in(key_list[6], 71), 0)
    weight = normal_values(key_list[5], (F, F), F ** -0.5, 0.1875, ((1, 8),))
    return {"sources": sources, "adjacency": adjacency, "target_block": target_block, "source_block": source_block, "slot_counts": slot_counts, "weight": weight}


def reference(sources, adjacency, target_block, source_block, slot_counts, weight):
    blocks_all = sources.reshape(NSTRIPE, SRC_DEV // BLOCK, BLOCK, F)

    def add_stripe(running, packed):
        adj_stripe, rows_stripe, cols_stripe, counts_stripe, blocks = packed

        def one_piece(adj_piece, rows_piece, cols_piece, count_piece):
            gathered = blocks[cols_piece].astype(jnp.float32)
            product = jnp.einsum("sij,sjf->sif", adj_piece.astype(jnp.float32), gathered)
            live_mask = (jnp.arange(SLOTS) < count_piece).astype(jnp.float32)
            summed = jax.ops.segment_sum(product * live_mask[:, None, None], rows_piece, num_segments=TGT_DEV // BLOCK)
            return summed.reshape(TGT_DEV, F)

        return running + jax.vmap(one_piece)(adj_stripe, rows_stripe, cols_stripe, counts_stripe), None

    initial = jnp.zeros((NSTRIPE, TGT_DEV, F), jnp.float32)
    aggregated, _ = lax.scan(add_stripe, initial, (adjacency, target_block, source_block, slot_counts, blocks_all))
    hidden = aggregated.reshape(TGT, F).astype(jnp.bfloat16)
    projected = jnp.dot(hidden, weight, preferred_element_type=jnp.float32)
    return jax.nn.relu(projected).astype(jnp.bfloat16)
```

```python
import functools

import jax
import jax.numpy as jnp
from jax import lax
from jax.experimental import pallas as pl
from jax.experimental.pallas import tpu as pltpu
from jax.sharding import PartitionSpec as P

BLOCK = 128
TGT_DEV = 1024
UNROLL = 4


def aggregate_kernel(target_ref, source_ref, count_ref, adj_ref, blocks_ref, out_ref, total_ref):
    piece = pl.program_id(0)
    block_total = TGT_DEV // BLOCK
    count = count_ref[piece]
    total_ref[...] = jnp.zeros_like(total_ref)

    def group(step, carry):
        products = []
        for u in range(UNROLL):
            slot = step * UNROLL + u
            products.append(
                jnp.dot(
                    adj_ref[0, slot],
                    blocks_ref[source_ref[piece, slot]],
                    preferred_element_type=jnp.float32,
                )
            )
        for u in range(UNROLL):
            slot = step * UNROLL + u
            row = jnp.where(slot < count, target_ref[piece, slot], block_total)
            total_ref[row] += products[u]
        return carry

    lax.fori_loop(0, (count + UNROLL - 1) // UNROLL, group, 0)
    out_ref[0] = total_ref[:block_total].reshape(TGT_DEV, BLOCK)


def aggregate(target, source, count, adj, blocks):
    pieces, slots = target.shape
    return pl.pallas_call(
        aggregate_kernel,
        out_shape=jax.ShapeDtypeStruct((pieces, TGT_DEV, blocks.shape[2]), jnp.float32),
        grid_spec=pltpu.PrefetchScalarGridSpec(
            num_scalar_prefetch=3,
            grid=(pieces,),
            in_specs=[
                pl.BlockSpec((1, slots, BLOCK, BLOCK), lambda p, *_: (p, 0, 0, 0)),
                pl.BlockSpec(memory_space=pltpu.VMEM),
            ],
            out_specs=pl.BlockSpec((1, TGT_DEV, blocks.shape[2]), lambda p, *_: (p, 0, 0)),
            scratch_shapes=[pltpu.VMEM((TGT_DEV // BLOCK + 1, BLOCK, blocks.shape[2]), jnp.float32)],
        ),
        compiler_params=pltpu.CompilerParams(vmem_limit_bytes=32 << 20),
        name="aggregate",
    )(target, source, count, adj, blocks)


def body(sources, adjacency, target_block, source_block, slot_counts, weight):
    feat_width = sources.shape[1]
    blocks = sources.reshape(sources.shape[0] // BLOCK, BLOCK, feat_width)
    piece_terms = aggregate(target_block[0], source_block[0], slot_counts[0], adjacency[0], blocks)
    summed = lax.psum_scatter(
        piece_terms.reshape(TGT_DEV * lax.axis_size(("blk", "sub")), feat_width),
        ("blk", "sub"),
        scatter_dimension=0,
        tiled=True,
    )
    hidden = summed.astype(jnp.bfloat16)
    projected = jnp.dot(
        lax.all_gather(hidden, "feat", axis=1, tiled=True),
        weight,
        preferred_element_type=jnp.float32,
    )
    return jax.nn.relu(projected).astype(jnp.bfloat16)


def solution(mesh):
    return jax.shard_map(
        body,
        mesh=mesh,
        in_specs=(
            P(("blk", "sub"), "feat"),
            P(("blk", "sub"), None, None, None, None),
            P(("blk", "sub"), None, None),
            P(("blk", "sub"), None, None),
            P(("blk", "sub"), None),
            P(None, "feat"),
        ),
        out_specs=P(("blk", "sub"), "feat"),
        check_vma=False,
    )
```

```python
import jax
import jax.numpy as jnp
from jax import lax
from jax.experimental import pallas as pl
from jax.experimental.pallas import tpu as pltpu
from jax.sharding import PartitionSpec as P

BLOCK = 128
TGT_DEV = 1024
UNROLL = 8
RING = 4
CHUNKS = (128,) * 8
MESH = pl.DeviceIdType.MESH


def aggregate_kernel(core_ref, target_ref, source_ref, count_ref, adj_ref, blocks_ref, out_ref, total_ref):
    piece = pl.program_id(0)
    block_total = TGT_DEV // BLOCK
    count = count_ref[piece]
    total_ref[...] = jnp.zeros_like(total_ref)

    def group(step, carry):
        products = []
        for u in range(UNROLL):
            slot = step * UNROLL + u
            products.append(
                jnp.dot(
                    adj_ref[0, slot],
                    blocks_ref[source_ref[piece, slot]],
                    preferred_element_type=jnp.float32,
                )
            )
        for u in range(UNROLL):
            slot = step * UNROLL + u
            row = jnp.where(slot < count, target_ref[piece, slot], block_total)
            total_ref[row] += products[u]
        return carry

    lax.fori_loop(0, (count + UNROLL - 1) // UNROLL, group, 0)
    out_ref[0] = total_ref[:block_total].reshape(TGT_DEV, BLOCK).astype(out_ref.dtype)


def aggregate(core, target, source, count, adj, blocks):
    pieces, slots = target.shape

    def placed(p, core_ref, *_):
        return ((p // RING) * (RING - core_ref[0] * (RING - 1)) + (p % RING) * (1 + core_ref[0] * (RING - 1)), 0, 0)

    return pl.pallas_call(
        aggregate_kernel,
        out_shape=jax.ShapeDtypeStruct((pieces, TGT_DEV, blocks.shape[2]), jnp.bfloat16),
        grid_spec=pltpu.PrefetchScalarGridSpec(
            num_scalar_prefetch=4,
            grid=(pieces,),
            in_specs=[
                pl.BlockSpec((1, slots, BLOCK, BLOCK), lambda p, *_: (p, 0, 0, 0)),
                pl.BlockSpec(memory_space=pltpu.VMEM),
            ],
            out_specs=pl.BlockSpec((1, TGT_DEV, blocks.shape[2]), placed),
            scratch_shapes=[pltpu.VMEM((TGT_DEV // BLOCK + 1, BLOCK, blocks.shape[2]), jnp.float32)],
        ),
        compiler_params=pltpu.CompilerParams(vmem_limit_bytes=40 << 20),
        name="aggregate",
    )(core, target, source, count, adj, blocks)


F1, C1, P1, F2, C2, P2, Z1, Z2, OWN, FWD1, FWD2 = range(0, 22, 2)
KINDS = 22


def exchange_kernel(
    part, weight_ref, out_ref, got1, mix1, row32, row16, got2, mix2, hidden, send_sems, recv_sems
):
    blk, sub, feat = lax.axis_index("blk"), lax.axis_index("sub"), lax.axis_index("feat")
    x, y = blk // 2, (blk % 2) * 2 + sub
    z, core = feat // 2, feat % 2
    ia = x * (1 - core) + y * core
    ib = y * (1 - core) + x * core

    def at(ja, jb, jz, jcore):
        px = ja * (1 - core) + jb * core
        py = jb * (1 - core) + ja * core
        return (px * 2 + py // 2, py % 2, jz * 2 + jcore)

    step = (1, RING - 1)
    near_a = [(ia + s) % RING for s in step]
    near_b = [(ib + s) % RING for s in step]
    near_z = [(z + s) % RING for s in step]
    dev_a = [at(j, ib, z, core) for j in near_a]
    dev_b = [at(ia, j, z, core) for j in near_b]
    dev_z = [at(ia, ib, j, core) for j in near_z]
    mate = (blk, sub, z * 2 + 1 - core)
    far_a, far_b = (ia + 2) % RING, (ib + 2) % RING

    barrier = pltpu.get_barrier_semaphore()
    everyone = dev_a + dev_b + dev_z + [mate]
    for device in everyone:
        pl.semaphore_signal(barrier, inc=1, device_id=device, device_id_type=MESH)
    pl.semaphore_wait(barrier, len(everyone))

    starts = [sum(CHUNKS[:c]) for c in range(len(CHUNKS))]

    def rows(c, half=None):
        n = CHUNKS[c]
        if half is None:
            return pl.ds(starts[c], n)
        return pl.ds(starts[c] + half * (n // 2), n // 2)

    def packed(c):
        return pl.ds(starts[c] // 2, CHUNKS[c] // 2)

    def copy(kind, c, src, dst, device):
        return pltpu.make_async_remote_copy(
            src_ref=src,
            dst_ref=dst,
            send_sem=send_sems.at[kind, c],
            recv_sem=recv_sems.at[kind, c],
            device_id=device,
            device_id_type=MESH,
        )

    def first(kind, c, d):
        if kind == F1:
            src = part.at[far_a, :, rows(c, d)]
        elif kind == P1:
            src = part.at[near_a[d], :, rows(c, 1 - d)]
        else:
            src = mix1.at[d, :, packed(c)]
        return copy(kind + d, c, src, got1.at[kind // 2, d, :, packed(c)], dev_a[d])

    def second(kind, c, d):
        if kind == F2:
            src = row16.at[far_b, rows(c, d)]
        elif kind == P2:
            src = row16.at[near_b[d], rows(c, 1 - d)]
        else:
            src = mix2.at[d, packed(c)]
        return copy(kind + d, c, src, got2.at[(kind - F2) // 2, d, packed(c)], dev_b[d])

    def along_z(c, d):
        here = hidden.at[feat, rows(c)]
        return copy(Z1 + d, c, here, here, dev_z[d])

    def relay_z(c, d):
        here = hidden.at[near_z[1 - d] * 2 + core, rows(c, d)]
        return copy(Z2 + d, c, here, here, dev_z[d])

    def to_mate(kind, c, which):
        f = ((z + which) % RING) * 2 + core
        here = hidden.at[f, rows(c)]
        return copy(kind, c, here, here, mate)

    def mate_copies(c):
        return [to_mate(OWN, c, 0), to_mate(FWD1, c, 1), to_mate(FWD1 + 1, c, 3), to_mate(FWD2, c, 2)]

    def send_far1(c):
        for d in (0, 1):
            first(F1, c, d).start()

    def send_plain1(c):
        for d in (0, 1):
            first(P1, c, d).start()

    def stage1(c):
        for d in (0, 1):
            first(F1, c, d).wait_recv()

            def add(jb, carry):
                mix1[d, jb, packed(c)] = (
                    part[near_a[d], jb, rows(c, d)].astype(jnp.float32)
                    + got1[0, d, jb, packed(c)].astype(jnp.float32)
                ).astype(jnp.bfloat16)
                return carry

            lax.fori_loop(0, RING, add, 0)
            first(C1, c, d).start()

    def stage2(c):
        for d in (0, 1):
            first(C1, c, d).wait_recv()
            first(P1, c, d).wait_recv()

        def add(jb, carry):
            for d in (0, 1):
                value = (
                    part[ia, jb, rows(c, d)].astype(jnp.float32)
                    + got1[1, d, jb, packed(c)].astype(jnp.float32)
                    + got1[2, 1 - d, jb, packed(c)].astype(jnp.float32)
                )
                row32[jb, rows(c, d)] = value
                row16[jb, rows(c, d)] = value.astype(jnp.bfloat16)
            return carry

        lax.fori_loop(0, RING, add, 0)
        for d in (0, 1):
            second(F2, c, d).start()
        for d in (0, 1):
            second(P2, c, d).start()

    def stage3(c):
        for d in (0, 1):
            second(F2, c, d).wait_recv()
            mix2[d, packed(c)] = (
                row32[near_b[d], rows(c, d)] + got2[0, d, packed(c)].astype(jnp.float32)
            ).astype(jnp.bfloat16)
            second(C2, c, d).start()

    def stage4(c):
        for d in (0, 1):
            second(C2, c, d).wait_recv()
            second(P2, c, d).wait_recv()
        for d in (0, 1):
            hidden[feat, rows(c, d)] = (
                row32[ib, rows(c, d)]
                + got2[1, d, packed(c)].astype(jnp.float32)
                + got2[2, 1 - d, packed(c)].astype(jnp.float32)
            ).astype(jnp.bfloat16)
        for d in (0, 1):
            along_z(c, d).start()
        to_mate(OWN, c, 0).start()

    def stage5(c):
        for d in (0, 1):
            along_z(c, d).wait_recv()
            relay_z(c, d).start()
        to_mate(FWD1, c, 1).start()
        to_mate(FWD1 + 1, c, 3).start()

    def stage6(c):
        for d in (0, 1):
            relay_z(c, d).wait_recv()
        to_mate(FWD2, c, 2).start()

    def stage7(c):
        for m in mate_copies(c):
            m.wait_recv()
        total = jnp.zeros((CHUNKS[c], BLOCK), jnp.float32)
        for f in range(2 * RING):
            total += jnp.dot(
                hidden[f, rows(c)],
                weight_ref[f * BLOCK : (f + 1) * BLOCK, :],
                preferred_element_type=jnp.float32,
            )
        out_ref[rows(c), :] = jnp.maximum(total, 0.0).astype(out_ref.dtype)

    n = len(CHUNKS)
    send_far1(0)
    send_plain1(0)
    send_far1(1)
    stages = (stage1, stage2, stage3, stage4, stage5, stage6, stage7)
    for t in range(n + len(stages) - 1):
        for lag, stage in enumerate(stages):
            c = t - lag
            if 0 <= c < n:
                stage(c)
            if lag == 0:
                if t + 1 < n:
                    send_plain1(t + 1)
                if t + 2 < n:
                    send_far1(t + 2)

    for c in range(n):
        for d in (0, 1):
            for kind in (F1, C1, P1):
                first(kind, c, d).wait_send()
            for kind in (F2, C2, P2):
                second(kind, c, d).wait_send()
            along_z(c, d).wait_send()
            relay_z(c, d).wait_send()
        for m in mate_copies(c):
            m.wait_send()


def exchange(part, weight):
    half = TGT_DEV // 2
    vmem = pl.BlockSpec(memory_space=pltpu.VMEM)
    return pl.pallas_call(
        exchange_kernel,
        out_shape=jax.ShapeDtypeStruct((TGT_DEV, BLOCK), jnp.bfloat16),
        in_specs=[vmem, vmem],
        out_specs=vmem,
        scratch_shapes=[
            pltpu.VMEM((3, 2, RING, half, BLOCK), jnp.bfloat16),
            pltpu.VMEM((2, RING, half, BLOCK), jnp.bfloat16),
            pltpu.VMEM((RING, TGT_DEV, BLOCK), jnp.float32),
            pltpu.VMEM((RING, TGT_DEV, BLOCK), jnp.bfloat16),
            pltpu.VMEM((3, 2, half, BLOCK), jnp.bfloat16),
            pltpu.VMEM((2, half, BLOCK), jnp.bfloat16),
            pltpu.VMEM((2 * RING, TGT_DEV, BLOCK), jnp.bfloat16),
            pltpu.SemaphoreType.DMA((KINDS, len(CHUNKS))),
            pltpu.SemaphoreType.DMA((KINDS, len(CHUNKS))),
        ],
        compiler_params=pltpu.CompilerParams(
            collective_id=0, has_side_effects=True, vmem_limit_bytes=32 << 20
        ),
        name="exchange",
    )(part, weight)


def body(sources, adjacency, target_block, source_block, slot_counts, weight):
    feat_width = sources.shape[1]
    blocks = sources.reshape(sources.shape[0] // BLOCK, BLOCK, feat_width)
    core = (lax.axis_index("feat") % 2).astype(jnp.int32).reshape(1)
    part = aggregate(core, target_block[0], source_block[0], slot_counts[0], adjacency[0], blocks)
    return exchange(part.reshape(RING, RING, TGT_DEV, feat_width), weight)


def solution(mesh):
    return jax.shard_map(
        body,
        mesh=mesh,
        in_specs=(
            P(("blk", "sub"), "feat"),
            P(("blk", "sub"), None, None, None, None),
            P(("blk", "sub"), None, None),
            P(("blk", "sub"), None, None),
            P(("blk", "sub"), None),
            P(None, "feat"),
        ),
        out_specs=P(("blk", "sub"), "feat"),
        check_vma=False,
    )
```

```python
import jax
import jax.numpy as jnp
from jax import lax
from jax.experimental import pallas as pl
from jax.experimental.pallas import tpu as pltpu
from jax.sharding import PartitionSpec as P

BLOCK = 128
TGT_DEV = 1024
SLOTS = 32
RING = 4
PIECES = RING * RING
TARGETS = TGT_DEV // BLOCK
UNROLL = 16
CHUNKS = (64,) * 8
DIRECT = (7,)
LAGS = (0, 2, 4, 6, 8, 9)
MESH = pl.DeviceIdType.MESH

F1, C1, P1, F2, C2, P2, ZNEAR = range(0, 14, 2)
ZFAR, OWN, FWD0, FWD1, FWD2 = range(14, 19)
KINDS = 19

ORDER, SOURCE, KEEP, LAST = 0, SLOTS, 2 * SLOTS, 3 * SLOTS


def slot_table(target, source, count_ref, table):
    shape = target.shape
    row = lax.broadcasted_iota(jnp.int32, shape, 0)
    lane = lax.broadcasted_iota(jnp.int32, shape, 1)
    count = jnp.zeros(shape, jnp.int32)
    for p in range(PIECES):
        count = jnp.where(row == p, count_ref[0, p], count)
    key = jnp.where(lane < count, target, TARGETS)
    unique = key * SLOTS + lane
    rank = jnp.zeros(shape, jnp.int32)
    earlier = jnp.zeros(shape, jnp.int32)
    upto = jnp.zeros(shape, jnp.int32)
    hit = jnp.zeros(shape, jnp.int32)
    for j in range(SLOTS):
        key_j = jnp.broadcast_to(key[:, j : j + 1], shape)
        rank += jnp.where(key_j * SLOTS + j < unique, 1, 0)
        earlier += jnp.where((key_j == key) & (lane > j), 1, 0)
        upto += jnp.where(key_j <= lane, 1, 0)
        hit += jnp.where(key_j == lane, 1, 0)
    keep = jnp.where(earlier > 0, 1, 0)
    order = jnp.zeros(shape, jnp.int32)
    source_of = jnp.zeros(shape, jnp.int32)
    keep_of = jnp.zeros(shape, jnp.int32)
    for k in range(SLOTS):
        here = jnp.broadcast_to(rank[:, k : k + 1], shape) == lane
        order = jnp.where(here, k, order)
        source_of = jnp.where(here, jnp.broadcast_to(source[:, k : k + 1], shape), source_of)
        keep_of = jnp.where(here, jnp.broadcast_to(keep[:, k : k + 1], shape), keep_of)
    table[:, ORDER : ORDER + SLOTS] = order
    table[:, SOURCE : SOURCE + SLOTS] = source_of
    table[:, KEEP : KEEP + SLOTS] = keep_of
    table[:, LAST : LAST + SLOTS] = jnp.where(hit > 0, upto - 1, SLOTS)


def layer_kernel(
    target_hbm, source_hbm, count_hbm, adj_hbm, blocks_hbm, weight_hbm, out_ref, *scratch
):
    (target_ref, source_ref, count_ref, table_ref, table, blocks, weight_ref, sums, part, got1, mix1,
     row32, row16, got2, mix2, gotd, hidden, load_sems, adj_sems, send_sems, recv_sems) = scratch[:21]
    tiles = scratch[21:]

    blk, sub, feat = lax.axis_index("blk"), lax.axis_index("sub"), lax.axis_index("feat")
    x, y = blk // 2, (blk % 2) * 2 + sub
    z, core = feat // 2, feat % 2
    ia = x * (1 - core) + y * core
    ib = y * (1 - core) + x * core

    def at(ja, jb, jz, jcore):
        px = ja * (1 - core) + jb * core
        py = jb * (1 - core) + ja * core
        return (px * 2 + py // 2, py % 2, jz * 2 + jcore)

    step = (1, RING - 1)
    near_a = [(ia + s) % RING for s in step]
    near_b = [(ib + s) % RING for s in step]
    near_z = [(z + s) % RING for s in step]
    far_a, far_b, far_z = (ia + 2) % RING, (ib + 2) % RING, (z + 2) % RING
    dev_a = [at(j, ib, z, core) for j in near_a]
    dev_b = [at(ia, j, z, core) for j in near_b]
    dev_z = [at(ia, ib, j, core) for j in near_z]
    dev_b_far = at(ia, far_b, z, core)
    dev_z_far = at(ia, ib, far_z, core)
    mate = (blk, sub, z * 2 + 1 - core)

    small = [
        pltpu.make_async_copy(target_hbm, target_ref, load_sems.at[0]),
        pltpu.make_async_copy(source_hbm, source_ref, load_sems.at[1]),
        pltpu.make_async_copy(count_hbm, count_ref, load_sems.at[2]),
    ]
    for load in small:
        load.start()
    quarter = blocks.shape[0] // 4
    block_loads = [
        pltpu.make_async_copy(
            blocks_hbm.at[pl.ds(q * quarter, quarter)], blocks.at[pl.ds(q * quarter, quarter)], load_sems.at[3 + q]
        )
        for q in range(4)
    ]
    for load in block_loads:
        load.start()
    places = [(ja, jb) for ja in (far_a, near_a[0], near_a[1], ia) for jb in (0, 1, 2, 3)]

    def number(ja, jb):
        return (ja * (1 - core) + jb * core) * RING + jb * (1 - core) + ja * core

    tile_loads = [
        pltpu.make_async_copy(adj_hbm.at[number(ja, jb)], tiles[i], adj_sems.at[i])
        for i, (ja, jb) in enumerate(places)
    ]
    for load in tile_loads:
        load.start()
    weight_load = pltpu.make_async_copy(weight_hbm, weight_ref, load_sems.at[7])
    weight_load.start()

    barrier = pltpu.get_barrier_semaphore()
    everyone = dev_a + dev_b + dev_z + [dev_b_far, dev_z_far, mate]
    for device in everyone:
        pl.semaphore_signal(barrier, inc=1, device_id=device, device_id_type=MESH)

    sums[SLOTS] = jnp.zeros((BLOCK, BLOCK), jnp.float32)
    for load in small:
        load.wait()
    slot_table(target_ref[...], source_ref[...], count_ref, table_ref)
    to_scalars = pltpu.make_async_copy(table_ref, table, load_sems.at[8])
    to_scalars.start()
    to_scalars.wait()
    for load in block_loads:
        load.wait()

    def compute(i):
        tile_loads[i].wait()
        ja, jb = places[i]
        p = number(ja, jb)

        def group(g, total):
            products = []
            for u in range(UNROLL):
                slot = g * UNROLL + u
                products.append(
                    jnp.dot(
                        tiles[i][table[p, ORDER + slot]],
                        blocks[table[p, SOURCE + slot]],
                        preferred_element_type=jnp.float32,
                    )
                )
            for u in range(UNROLL):
                slot = g * UNROLL + u
                total = total * table[p, KEEP + slot].astype(jnp.float32) + products[u]
                sums[slot] = total
            return total

        lax.fori_loop(0, SLOTS // UNROLL, group, jnp.zeros((BLOCK, BLOCK), jnp.float32))
        for t in range(TARGETS):
            value = sums[table[p, LAST + t]]
            if i < 12:
                part[ja, jb, t // 4, (t % 4) * BLOCK : (t % 4 + 1) * BLOCK] = value.astype(jnp.bfloat16)
            else:
                row32[jb, t // 4, (t % 4) * BLOCK : (t % 4 + 1) * BLOCK] = value

    starts = [sum(CHUNKS[:c]) for c in range(len(CHUNKS))]

    def rows(c):
        return pl.ds(starts[c], CHUNKS[c])

    def copy(kind, c, src, dst, device):
        return pltpu.make_async_remote_copy(
            src_ref=src,
            dst_ref=dst,
            send_sem=send_sems.at[kind, c],
            recv_sem=recv_sems.at[kind, c],
            device_id=device,
            device_id_type=MESH,
        )

    def far1(jb, d):
        return copy(F1 + d, jb, part.at[far_a, jb, d], got1.at[0, d, jb], dev_a[d])

    def first(kind, c, d):
        if kind == P1:
            src = part.at[near_a[d], :, 1 - d, rows(c)]
        else:
            src = mix1.at[d, :, rows(c)]
        return copy(kind + d, c, src, got1.at[kind // 2, d, :, rows(c)], dev_a[d])

    def second(kind, c, d):
        if kind == F2:
            src = row16.at[far_b, d, rows(c)]
        elif kind == P2:
            src = row16.at[near_b[d], 1 - d, rows(c)]
        else:
            src = mix2.at[d, rows(c)]
        return copy(kind + d, c, src, got2.at[(kind - F2) // 2, d, rows(c)], dev_b[d])

    def straight(c):
        return [
            copy(C2 + d, c, row16.at[near_b[d], :, rows(c)], gotd.at[d, :, rows(c)], dev_b[d]) for d in (0, 1)
        ] + [copy(F2, c, row16.at[far_b, :, rows(c)], gotd.at[2, :, rows(c)], dev_b_far)]

    def along_z(c):
        here = hidden.at[feat, :, rows(c)]
        return [copy(ZNEAR + d, c, here, here, dev_z[d]) for d in (0, 1)] + [copy(ZFAR, c, here, here, dev_z_far)]

    def to_mate(kind, c, chip):
        here = hidden.at[chip * 2 + core, :, rows(c)]
        return copy(kind, c, here, here, mate)

    def mate_copies(c):
        return [
            to_mate(OWN, c, z),
            to_mate(FWD0, c, near_z[0]),
            to_mate(FWD1, c, near_z[1]),
            to_mate(FWD2, c, far_z),
        ]

    def stage1(c):
        for d in (0, 1):
            for jb in range(RING):
                if c == 0:
                    far1(jb, d).wait_recv()

            def add(jb, carry):
                mix1[d, jb, rows(c)] = (
                    part[near_a[d], jb, d, rows(c)].astype(jnp.float32)
                    + got1[0, d, jb, rows(c)].astype(jnp.float32)
                ).astype(jnp.bfloat16)
                return carry

            lax.fori_loop(0, RING, add, 0)
            first(C1, c, d).start()
        for d in (0, 1):
            first(P1, c, d).start()

    def stage2(c):
        for d in (0, 1):
            first(C1, c, d).wait_recv()
            first(P1, c, d).wait_recv()

        def add(jb, carry):
            for d in (0, 1):
                value = (
                    row32[jb, d, rows(c)]
                    + got1[1, d, jb, rows(c)].astype(jnp.float32)
                    + got1[2, 1 - d, jb, rows(c)].astype(jnp.float32)
                )
                row32[jb, d, rows(c)] = value
                row16[jb, d, rows(c)] = value.astype(jnp.bfloat16)
            return carry

        lax.fori_loop(0, RING, add, 0)
        if c in DIRECT:
            for s in straight(c):
                s.start()
        else:
            for d in (0, 1):
                second(F2, c, d).start()
            for d in (0, 1):
                second(P2, c, d).start()

    def stage3(c):
        if c in DIRECT:
            return
        for d in (0, 1):
            second(F2, c, d).wait_recv()
            mix2[d, rows(c)] = (
                row32[near_b[d], d, rows(c)] + got2[0, d, rows(c)].astype(jnp.float32)
            ).astype(jnp.bfloat16)
            second(C2, c, d).start()

    def stage4(c):
        if c in DIRECT:
            for s in straight(c):
                s.wait_recv()
            for d in (0, 1):
                hidden[feat, d, rows(c)] = (
                    row32[ib, d, rows(c)]
                    + gotd[0, d, rows(c)].astype(jnp.float32)
                    + gotd[1, d, rows(c)].astype(jnp.float32)
                    + gotd[2, d, rows(c)].astype(jnp.float32)
                ).astype(jnp.bfloat16)
        else:
            for d in (0, 1):
                second(C2, c, d).wait_recv()
                second(P2, c, d).wait_recv()
            for d in (0, 1):
                hidden[feat, d, rows(c)] = (
                    row32[ib, d, rows(c)]
                    + got2[1, d, rows(c)].astype(jnp.float32)
                    + got2[2, 1 - d, rows(c)].astype(jnp.float32)
                ).astype(jnp.bfloat16)
        for s in along_z(c):
            s.start()
        to_mate(OWN, c, z).start()

    def stage5(c):
        for s, kind, chip in zip(along_z(c), (FWD1, FWD0, FWD2), (near_z[1], near_z[0], far_z)):
            s.wait_recv()
            to_mate(kind, c, chip).start()

    def stage6(c):
        if c == 0:
            weight_load.wait()
        for m in mate_copies(c):
            m.wait_recv()
        total = jnp.zeros((2 * CHUNKS[c], BLOCK), jnp.float32)
        for f in range(2 * RING):
            total += jnp.dot(
                hidden[f, :, rows(c)].reshape(2 * CHUNKS[c], BLOCK),
                weight_ref[f * BLOCK : (f + 1) * BLOCK, :],
                preferred_element_type=jnp.float32,
            )
        value = jnp.maximum(total, 0.0).astype(out_ref.dtype)
        for d in (0, 1):
            out_ref[d, rows(c)] = value[d * CHUNKS[c] : (d + 1) * CHUNKS[c]]

    n = len(CHUNKS)
    for i in range(PIECES):
        compute(i)
        if i == 0:
            pl.semaphore_wait(barrier, len(everyone))
        if i < RING:
            for d in (0, 1):
                far1(i, d).start()
    stages = (stage1, stage2, stage3, stage4, stage5, stage6)
    for t in range(n + LAGS[-1]):
        for lag, stage in zip(LAGS, stages):
            if 0 <= t - lag < n:
                stage(t - lag)

    for d in (0, 1):
        for jb in range(RING):
            far1(jb, d).wait_send()
    for c in range(n):
        for d in (0, 1):
            for kind in (C1, P1):
                first(kind, c, d).wait_send()
        if c in DIRECT:
            for s in straight(c):
                s.wait_send()
        else:
            for d in (0, 1):
                for kind in (F2, C2, P2):
                    second(kind, c, d).wait_send()
        for s in along_z(c) + mate_copies(c):
            s.wait_send()


def layer(target, source, count, adj, blocks, weight):
    half = TGT_DEV // 2
    n = len(CHUNKS)
    hbm = pl.BlockSpec(memory_space=pltpu.HBM)
    bf16, f32 = jnp.bfloat16, jnp.float32
    return pl.pallas_call(
        layer_kernel,
        out_shape=jax.ShapeDtypeStruct((2, half, BLOCK), bf16),
        in_specs=[hbm] * 6,
        out_specs=pl.BlockSpec(memory_space=pltpu.VMEM),
        scratch_shapes=[
            pltpu.VMEM(target.shape, jnp.int32),
            pltpu.VMEM(source.shape, jnp.int32),
            pltpu.SMEM(count.shape, jnp.int32),
            pltpu.VMEM((PIECES, 4 * SLOTS), jnp.int32),
            pltpu.SMEM((PIECES, 4 * SLOTS), jnp.int32),
            pltpu.VMEM(blocks.shape, bf16),
            pltpu.VMEM(weight.shape, bf16),
            pltpu.VMEM((SLOTS + 1, BLOCK, BLOCK), f32),
            pltpu.VMEM((RING, RING, 2, half, BLOCK), bf16),
            pltpu.VMEM((3, 2, RING, half, BLOCK), bf16),
            pltpu.VMEM((2, RING, half, BLOCK), bf16),
            pltpu.VMEM((RING, 2, half, BLOCK), f32),
            pltpu.VMEM((RING, 2, half, BLOCK), bf16),
            pltpu.VMEM((3, 2, half, BLOCK), bf16),
            pltpu.VMEM((2, half, BLOCK), bf16),
            pltpu.VMEM((3, 2, half, BLOCK), bf16),
            pltpu.VMEM((2 * RING, 2, half, BLOCK), bf16),
            pltpu.SemaphoreType.DMA((9,)),
            pltpu.SemaphoreType.DMA((PIECES,)),
            pltpu.SemaphoreType.DMA((KINDS, n)),
            pltpu.SemaphoreType.DMA((KINDS, n)),
        ]
        + [pltpu.VMEM(adj.shape[1:], bf16) for _ in range(PIECES)],
        compiler_params=pltpu.CompilerParams(
            collective_id=0, has_side_effects=True, vmem_limit_bytes=56 << 20
        ),
        name="layer",
    )(target, source, count, adj, blocks, weight).reshape(TGT_DEV, BLOCK)


def body(sources, adjacency, target_block, source_block, slot_counts, weight):
    blocks = sources.reshape(sources.shape[0] // BLOCK, BLOCK, sources.shape[1])
    return layer(target_block[0], source_block[0], slot_counts, adjacency[0], blocks, weight)


def solution(mesh):
    return jax.shard_map(
        body,
        mesh=mesh,
        in_specs=(
            P(("blk", "sub"), "feat"),
            P(("blk", "sub"), None, None, None, None),
            P(("blk", "sub"), None, None),
            P(("blk", "sub"), None, None),
            P(("blk", "sub"), None),
            P(None, "feat"),
        ),
        out_specs=P(("blk", "sub"), "feat"),
        check_vma=False,
    )
```

```python
import jax
import jax.numpy as jnp
from jax import lax
from jax.experimental import pallas as pl
from jax.experimental.pallas import tpu as pltpu
from jax.sharding import PartitionSpec as P

BLOCK = 128
TGT_DEV = 1024
SLOTS = 32
RING = 4
PIECES = RING * RING
TARGETS = TGT_DEV // BLOCK
UNROLL = 16
CHUNKS = (160, 160, 128, 64)
DIRECT = (0, 1, 2, 3)
AHEAD = 2
BOTH = (3,)
VMEM_LIMIT = 56 << 20
LAGS = (0, 4, 4, 5, 6, 7)
MESH = pl.DeviceIdType.MESH

F1, C1, P1, F2, C2, P2, ZNEAR = range(0, 14, 2)
ZFAR, OWN, FWD0, FWD1, FWD2 = range(14, 19)
KINDS = 19

ORDER, SOURCE, KEEP, LAST = 0, SLOTS, 2 * SLOTS, 3 * SLOTS


def slot_table(target, source, count_ref, table):
    shape = target.shape
    row = lax.broadcasted_iota(jnp.int32, shape, 0)
    lane = lax.broadcasted_iota(jnp.int32, shape, 1)
    count = jnp.zeros(shape, jnp.int32)
    for p in range(PIECES):
        count = jnp.where(row == p, count_ref[0, p], count)
    key = jnp.where(lane < count, target, TARGETS)
    unique = key * SLOTS + lane
    rank = jnp.zeros(shape, jnp.int32)
    earlier = jnp.zeros(shape, jnp.int32)
    upto = jnp.zeros(shape, jnp.int32)
    hit = jnp.zeros(shape, jnp.int32)
    for j in range(SLOTS):
        key_j = jnp.broadcast_to(key[:, j : j + 1], shape)
        rank += jnp.where(key_j * SLOTS + j < unique, 1, 0)
        earlier += jnp.where((key_j == key) & (lane > j), 1, 0)
        upto += jnp.where(key_j <= lane, 1, 0)
        hit += jnp.where(key_j == lane, 1, 0)
    keep = jnp.where(earlier > 0, 1, 0)
    order = jnp.zeros(shape, jnp.int32)
    source_of = jnp.zeros(shape, jnp.int32)
    keep_of = jnp.zeros(shape, jnp.int32)
    for k in range(SLOTS):
        here = jnp.broadcast_to(rank[:, k : k + 1], shape) == lane
        order = jnp.where(here, k, order)
        source_of = jnp.where(here, jnp.broadcast_to(source[:, k : k + 1], shape), source_of)
        keep_of = jnp.where(here, jnp.broadcast_to(keep[:, k : k + 1], shape), keep_of)
    table[:, ORDER : ORDER + SLOTS] = order
    table[:, SOURCE : SOURCE + SLOTS] = source_of
    table[:, KEEP : KEEP + SLOTS] = keep_of
    table[:, LAST : LAST + SLOTS] = jnp.where(hit > 0, upto - 1, SLOTS)


def layer_kernel(
    target_hbm, source_hbm, count_hbm, adj_hbm, blocks_hbm, weight_hbm, out_ref, *scratch
):
    (target_ref, source_ref, count_ref, table_ref, table, blocks, weight_ref, sums, part, got1, mix1,
     row32, row16, got2, mix2, gotd, hidden, load_sems, adj_sems, send_sems, recv_sems) = scratch[:21]
    tiles = scratch[21:]

    blk, sub, feat = lax.axis_index("blk"), lax.axis_index("sub"), lax.axis_index("feat")
    x, y = blk // 2, (blk % 2) * 2 + sub
    z, core = feat // 2, feat % 2
    ia = x * (1 - core) + y * core
    ib = y * (1 - core) + x * core

    def at(ja, jb, jz, jcore):
        px = ja * (1 - core) + jb * core
        py = jb * (1 - core) + ja * core
        return (px * 2 + py // 2, py % 2, jz * 2 + jcore)

    step = (1, RING - 1)
    near_a = [(ia + s) % RING for s in step]
    near_b = [(ib + s) % RING for s in step]
    near_z = [(z + s) % RING for s in step]
    far_a, far_b, far_z = (ia + 2) % RING, (ib + 2) % RING, (z + 2) % RING
    dev_a = [at(j, ib, z, core) for j in near_a]
    dev_b = [at(ia, j, z, core) for j in near_b]
    dev_z = [at(ia, ib, j, core) for j in near_z]
    dev_b_far = at(ia, far_b, z, core)
    dev_z_far = at(ia, ib, far_z, core)
    dev_other = [at(ia, ib, j, 1 - core) for j in (near_z[0], near_z[1], far_z)]
    mate = (blk, sub, z * 2 + 1 - core)

    small = [
        pltpu.make_async_copy(target_hbm, target_ref, load_sems.at[0]),
        pltpu.make_async_copy(source_hbm, source_ref, load_sems.at[1]),
        pltpu.make_async_copy(count_hbm, count_ref, load_sems.at[2]),
    ]
    for load in small:
        load.start()
    quarter = blocks.shape[0] // 4
    block_loads = [
        pltpu.make_async_copy(
            blocks_hbm.at[pl.ds(q * quarter, quarter)], blocks.at[pl.ds(q * quarter, quarter)], load_sems.at[3 + q]
        )
        for q in range(4)
    ]
    for load in block_loads:
        load.start()
    places = [(ja, jb) for ja in (far_a, near_a[0], near_a[1], ia) for jb in (0, 1, 2, 3)]

    def number(ja, jb):
        return (ja * (1 - core) + jb * core) * RING + jb * (1 - core) + ja * core

    tile_loads = [
        pltpu.make_async_copy(adj_hbm.at[number(ja, jb)], tiles[i], adj_sems.at[i])
        for i, (ja, jb) in enumerate(places)
    ]
    weight_load = pltpu.make_async_copy(weight_hbm, weight_ref, load_sems.at[7])

    barrier = pltpu.get_barrier_semaphore()
    everyone = dev_a + dev_b + dev_z + [dev_b_far, dev_z_far, mate] + dev_other
    for device in everyone:
        pl.semaphore_signal(barrier, inc=1, device_id=device, device_id_type=MESH)

    sums[SLOTS] = jnp.zeros((BLOCK, BLOCK), jnp.float32)
    for load in small:
        load.wait()
    for load in tile_loads + [weight_load]:
        load.start()
    slot_table(target_ref[...], source_ref[...], count_ref, table_ref)
    to_scalars = pltpu.make_async_copy(table_ref, table, load_sems.at[8])
    to_scalars.start()
    to_scalars.wait()
    for load in block_loads:
        load.wait()

    def compute(i):
        tile_loads[i].wait()
        ja, jb = places[i]
        p = number(ja, jb)

        def group(g, total):
            products = []
            for u in range(UNROLL):
                slot = g * UNROLL + u
                products.append(
                    jnp.dot(
                        tiles[i][table[p, ORDER + slot]],
                        blocks[table[p, SOURCE + slot]],
                        preferred_element_type=jnp.float32,
                    )
                )
            for u in range(UNROLL):
                slot = g * UNROLL + u
                total = total * table[p, KEEP + slot].astype(jnp.float32) + products[u]
                sums[slot] = total
            return total

        lax.fori_loop(0, SLOTS // UNROLL, group, jnp.zeros((BLOCK, BLOCK), jnp.float32))
        for t in range(TARGETS):
            value = sums[table[p, LAST + t]]
            if i < 12:
                part[ja, jb, t // 4, (t % 4) * BLOCK : (t % 4 + 1) * BLOCK] = value.astype(jnp.bfloat16)
            else:
                row32[jb, t // 4, (t % 4) * BLOCK : (t % 4 + 1) * BLOCK] = value

    n = len(CHUNKS)
    starts = [sum(CHUNKS[:c]) for c in range(n)]

    def rows(c):
        return pl.ds(starts[c], CHUNKS[c])

    def copy(kind, c, src, dst, device):
        return pltpu.make_async_remote_copy(
            src_ref=src,
            dst_ref=dst,
            send_sem=send_sems.at[kind, c],
            recv_sem=recv_sems.at[kind, c],
            device_id=device,
            device_id_type=MESH,
        )

    def far1(jb, d):
        return copy(F1 + d, jb, part.at[far_a, jb, d], got1.at[0, d, jb], dev_a[d])

    def first(kind, c, d):
        if kind == P1:
            src = part.at[near_a[d], :, 1 - d, rows(c)]
        else:
            src = mix1.at[d, :, rows(c)]
        return copy(kind + d, c, src, got1.at[kind // 2, d, :, rows(c)], dev_a[d])

    def second(kind, c, d):
        if kind == F2:
            src = row16.at[far_b, d, rows(c)]
        elif kind == P2:
            src = row16.at[near_b[d], 1 - d, rows(c)]
        else:
            src = mix2.at[d, rows(c)]
        return copy(kind + d, c, src, got2.at[(kind - F2) // 2, d, rows(c)], dev_b[d])

    def straight(c):
        return [
            copy(C2 + d, c, row16.at[near_b[d], :, rows(c)], gotd.at[d, :, rows(c)], dev_b[d]) for d in (0, 1)
        ] + [copy(F2, c, row16.at[far_b, :, rows(c)], gotd.at[2, :, rows(c)], dev_b_far)]

    def along_z(c):
        here = hidden.at[feat, :, rows(c)]
        return [copy(ZNEAR + d, c, here, here, dev_z[d]) for d in (0, 1)] + [copy(ZFAR, c, here, here, dev_z_far)]

    def to_mate(kind, c, chip):
        here = hidden.at[chip * 2 + core, :, rows(c)]
        return copy(kind, c, here, here, mate)

    def mate_copies(c):
        if c in BOTH:
            here = hidden.at[feat, :, rows(c)]
            return [to_mate(OWN, c, z)] + [
                copy(kind, c, here, here, device) for kind, device in zip((FWD0, FWD1, FWD2), dev_other)
            ]
        return [
            to_mate(OWN, c, z),
            to_mate(FWD0, c, near_z[0]),
            to_mate(FWD1, c, near_z[1]),
            to_mate(FWD2, c, far_z),
        ]

    def stage1(c):
        for d in (0, 1):
            for jb in range(RING):
                if c == 0:
                    far1(jb, d).wait_recv()

            def add(jb, carry):
                mix1[d, jb, rows(c)] = (
                    part[near_a[d], jb, d, rows(c)].astype(jnp.float32)
                    + got1[0, d, jb, rows(c)].astype(jnp.float32)
                ).astype(jnp.bfloat16)
                return carry

            lax.fori_loop(0, RING, add, 0)
            first(C1, c, d).start()
        if c + AHEAD < n:
            for d in (0, 1):
                first(P1, c + AHEAD, d).start()

    def stage2(c):
        for d in (0, 1):
            first(C1, c, d).wait_recv()
            first(P1, c, d).wait_recv()

        def add(jb, carry):
            for d in (0, 1):
                value = (
                    row32[jb, d, rows(c)]
                    + got1[1, d, jb, rows(c)].astype(jnp.float32)
                    + got1[2, 1 - d, jb, rows(c)].astype(jnp.float32)
                )
                row32[jb, d, rows(c)] = value
                row16[jb, d, rows(c)] = value.astype(jnp.bfloat16)
            return carry

        lax.fori_loop(0, RING, add, 0)
        if c in DIRECT:
            for s in straight(c):
                s.start()
        else:
            for d in (0, 1):
                second(F2, c, d).start()
            for d in (0, 1):
                second(P2, c, d).start()

    def stage3(c):
        if c in DIRECT:
            return
        for d in (0, 1):
            second(F2, c, d).wait_recv()
            mix2[d, rows(c)] = (
                row32[near_b[d], d, rows(c)] + got2[0, d, rows(c)].astype(jnp.float32)
            ).astype(jnp.bfloat16)
            second(C2, c, d).start()

    def stage4(c):
        if c in DIRECT:
            for s in straight(c):
                s.wait_recv()
            for d in (0, 1):
                hidden[feat, d, rows(c)] = (
                    row32[ib, d, rows(c)]
                    + gotd[0, d, rows(c)].astype(jnp.float32)
                    + gotd[1, d, rows(c)].astype(jnp.float32)
                    + gotd[2, d, rows(c)].astype(jnp.float32)
                ).astype(jnp.bfloat16)
        else:
            for d in (0, 1):
                second(C2, c, d).wait_recv()
                second(P2, c, d).wait_recv()
            for d in (0, 1):
                hidden[feat, d, rows(c)] = (
                    row32[ib, d, rows(c)]
                    + got2[1, d, rows(c)].astype(jnp.float32)
                    + got2[2, 1 - d, rows(c)].astype(jnp.float32)
                ).astype(jnp.bfloat16)
        for s in along_z(c):
            s.start()
        for s in mate_copies(c) if c in BOTH else [to_mate(OWN, c, z)]:
            s.start()

    def stage5(c):
        for s, kind, chip in zip(along_z(c), (FWD1, FWD0, FWD2), (near_z[1], near_z[0], far_z)):
            s.wait_recv()
            if c not in BOTH:
                to_mate(kind, c, chip).start()

    def stage6(c):
        if c == 0:
            weight_load.wait()
        for m in mate_copies(c):
            m.wait_recv()
        total = jnp.zeros((2 * CHUNKS[c], BLOCK), jnp.float32)
        for f in range(2 * RING):
            total += jnp.dot(
                hidden[f, :, rows(c)].reshape(2 * CHUNKS[c], BLOCK),
                weight_ref[f * BLOCK : (f + 1) * BLOCK, :],
                preferred_element_type=jnp.float32,
            )
        value = jnp.maximum(total, 0.0).astype(out_ref.dtype)
        for d in (0, 1):
            out_ref[d, rows(c)] = value[d * CHUNKS[c] : (d + 1) * CHUNKS[c]]

    for i in range(PIECES):
        compute(i)
        if i == 0:
            pl.semaphore_wait(barrier, len(everyone))
        if i < RING:
            for d in (0, 1):
                far1(i, d).start()
        if i in (2 * RING - 1, 3 * RING - 1):
            for c in range(AHEAD):
                first(P1, c, i // RING - 1).start()
    stages = (stage1, stage2, stage3, stage4, stage5, stage6)
    for t in range(n + LAGS[-1]):
        for lag, stage in zip(LAGS, stages):
            if 0 <= t - lag < n:
                stage(t - lag)

    for d in (0, 1):
        for jb in range(RING):
            far1(jb, d).wait_send()
    for c in range(n):
        for d in (0, 1):
            for kind in (C1, P1):
                first(kind, c, d).wait_send()
        if c in DIRECT:
            for s in straight(c):
                s.wait_send()
        else:
            for d in (0, 1):
                for kind in (F2, C2, P2):
                    second(kind, c, d).wait_send()
        for s in along_z(c) + mate_copies(c):
            s.wait_send()


def layer(target, source, count, adj, blocks, weight):
    half = TGT_DEV // 2
    n = len(CHUNKS)
    hbm = pl.BlockSpec(memory_space=pltpu.HBM)
    bf16, f32 = jnp.bfloat16, jnp.float32
    return pl.pallas_call(
        layer_kernel,
        out_shape=pltpu.VMEM((2, half, BLOCK), bf16),
        in_specs=[hbm] * 6,
        out_specs=pl.BlockSpec(memory_space=pltpu.VMEM),
        scratch_shapes=[
            pltpu.VMEM(target.shape, jnp.int32),
            pltpu.VMEM(source.shape, jnp.int32),
            pltpu.SMEM(count.shape, jnp.int32),
            pltpu.VMEM((PIECES, 4 * SLOTS), jnp.int32),
            pltpu.SMEM((PIECES, 4 * SLOTS), jnp.int32),
            pltpu.VMEM(blocks.shape, bf16),
            pltpu.VMEM(weight.shape, bf16),
            pltpu.VMEM((SLOTS + 1, BLOCK, BLOCK), f32),
            pltpu.VMEM((RING, RING, 2, half, BLOCK), bf16),
            pltpu.VMEM((3, 2, RING, half, BLOCK), bf16),
            pltpu.VMEM((2, RING, half, BLOCK), bf16),
            pltpu.VMEM((RING, 2, half, BLOCK), f32),
            pltpu.VMEM((RING, 2, half, BLOCK), bf16),
            pltpu.VMEM((3, 2, half, BLOCK), bf16),
            pltpu.VMEM((2, half, BLOCK), bf16),
            pltpu.VMEM((3, 2, half, BLOCK), bf16),
            pltpu.VMEM((2 * RING, 2, half, BLOCK), bf16),
            pltpu.SemaphoreType.DMA((9,)),
            pltpu.SemaphoreType.DMA((PIECES,)),
            pltpu.SemaphoreType.DMA((KINDS, n)),
            pltpu.SemaphoreType.DMA((KINDS, n)),
        ]
        + [pltpu.VMEM(adj.shape[1:], bf16) for _ in range(PIECES)],
        compiler_params=pltpu.CompilerParams(
            collective_id=0, has_side_effects=True, vmem_limit_bytes=VMEM_LIMIT
        ),
        name="layer",
    )(target, source, count, adj, blocks, weight).reshape(TGT_DEV, BLOCK)


def body(sources, adjacency, target_block, source_block, slot_counts, weight):
    blocks = sources.reshape(sources.shape[0] // BLOCK, BLOCK, sources.shape[1])
    return layer(target_block[0], source_block[0], slot_counts, adjacency[0], blocks, weight)


def solution(mesh):
    return jax.shard_map(
        body,
        mesh=mesh,
        in_specs=(
            P(("blk", "sub"), "feat"),
            P(("blk", "sub"), None, None, None, None),
            P(("blk", "sub"), None, None),
            P(("blk", "sub"), None, None),
            P(("blk", "sub"), None),
            P(None, "feat"),
        ),
        out_specs=P(("blk", "sub"), "feat"),
        check_vma=False,
    )
```

```python
import jax
import jax.numpy as jnp
from jax import lax
from jax.experimental import pallas as pl
from jax.experimental.pallas import tpu as pltpu
from jax.sharding import PartitionSpec as P

BLOCK = 128
TGT_DEV = 1024
SLOTS = 32
RING = 4
PIECES = RING * RING
TARGETS = TGT_DEV // BLOCK
UNROLL = 32
CHUNKS = (160, 160, 128, 64)
DIRECT = (0, 1, 2, 3)
AHEAD = 2
BOTH = (3,)
VMEM_LIMIT = 56 << 20
LAGS = (0, 4, 4, 5, 6, 7)
MESH = pl.DeviceIdType.MESH

F1, C1, P1, F2, C2, P2, ZNEAR = range(0, 14, 2)
ZFAR, OWN, FWD0, FWD1, FWD2 = range(14, 19)
KINDS = 19

ORDER, SOURCE, KEEP, LAST = 0, SLOTS, 2 * SLOTS, 3 * SLOTS


def slot_table(target, source, count_ref, table):
    shape = target.shape
    row = lax.broadcasted_iota(jnp.int32, shape, 0)
    lane = lax.broadcasted_iota(jnp.int32, shape, 1)
    count = jnp.zeros(shape, jnp.int32)
    for p in range(PIECES):
        count = jnp.where(row == p, count_ref[0, p], count)
    key = jnp.where(lane < count, target, TARGETS)
    unique = key * SLOTS + lane
    rank = jnp.zeros(shape, jnp.int32)
    earlier = jnp.zeros(shape, jnp.int32)
    upto = jnp.zeros(shape, jnp.int32)
    hit = jnp.zeros(shape, jnp.int32)
    for j in range(SLOTS):
        key_j = jnp.broadcast_to(key[:, j : j + 1], shape)
        rank += jnp.where(key_j * SLOTS + j < unique, 1, 0)
        earlier += jnp.where((key_j == key) & (lane > j), 1, 0)
        upto += jnp.where(key_j <= lane, 1, 0)
        hit += jnp.where(key_j == lane, 1, 0)
    keep = jnp.where(earlier > 0, 1, 0)
    order = jnp.zeros(shape, jnp.int32)
    source_of = jnp.zeros(shape, jnp.int32)
    keep_of = jnp.zeros(shape, jnp.int32)
    for k in range(SLOTS):
        here = jnp.broadcast_to(rank[:, k : k + 1], shape) == lane
        order = jnp.where(here, k, order)
        source_of = jnp.where(here, jnp.broadcast_to(source[:, k : k + 1], shape), source_of)
        keep_of = jnp.where(here, jnp.broadcast_to(keep[:, k : k + 1], shape), keep_of)
    table[:, ORDER : ORDER + SLOTS] = order
    table[:, SOURCE : SOURCE + SLOTS] = source_of
    table[:, KEEP : KEEP + SLOTS] = keep_of
    table[:, LAST : LAST + SLOTS] = jnp.where(hit > 0, upto - 1, SLOTS)


def layer_kernel(
    target_hbm, source_hbm, count_hbm, adj_hbm, blocks_hbm, weight_hbm, out_ref, *scratch
):
    (target_ref, source_ref, count_ref, table_ref, table, blocks, weight_ref, sums, part, got1, mix1,
     row32, row16, got2, mix2, gotd, hidden, load_sems, adj_sems, send_sems, recv_sems) = scratch[:21]
    tiles = scratch[21:]

    blk, sub, feat = lax.axis_index("blk"), lax.axis_index("sub"), lax.axis_index("feat")
    x, y = blk // 2, (blk % 2) * 2 + sub
    z, core = feat // 2, feat % 2
    ia = x * (1 - core) + y * core
    ib = y * (1 - core) + x * core

    def at(ja, jb, jz, jcore):
        px = ja * (1 - core) + jb * core
        py = jb * (1 - core) + ja * core
        return (px * 2 + py // 2, py % 2, jz * 2 + jcore)

    step = (1, RING - 1)
    near_a = [(ia + s) % RING for s in step]
    near_b = [(ib + s) % RING for s in step]
    near_z = [(z + s) % RING for s in step]
    far_a, far_b, far_z = (ia + 2) % RING, (ib + 2) % RING, (z + 2) % RING
    dev_a = [at(j, ib, z, core) for j in near_a]
    dev_b = [at(ia, j, z, core) for j in near_b]
    dev_z = [at(ia, ib, j, core) for j in near_z]
    dev_b_far = at(ia, far_b, z, core)
    dev_z_far = at(ia, ib, far_z, core)
    dev_other = [at(ia, ib, j, 1 - core) for j in (near_z[0], near_z[1], far_z)]
    mate = (blk, sub, z * 2 + 1 - core)

    small = [
        pltpu.make_async_copy(target_hbm, target_ref, load_sems.at[0]),
        pltpu.make_async_copy(source_hbm, source_ref, load_sems.at[1]),
        pltpu.make_async_copy(count_hbm, count_ref, load_sems.at[2]),
    ]
    for load in small:
        load.start()
    quarter = blocks.shape[0] // 4
    block_loads = [
        pltpu.make_async_copy(
            blocks_hbm.at[pl.ds(q * quarter, quarter)], blocks.at[pl.ds(q * quarter, quarter)], load_sems.at[3 + q]
        )
        for q in range(4)
    ]
    for load in block_loads:
        load.start()
    places = [(ja, jb) for ja in (far_a, near_a[0], near_a[1], ia) for jb in (0, 1, 2, 3)]

    def number(ja, jb):
        return (ja * (1 - core) + jb * core) * RING + jb * (1 - core) + ja * core

    tile_loads = [
        pltpu.make_async_copy(adj_hbm.at[number(ja, jb)], tiles[i], adj_sems.at[i])
        for i, (ja, jb) in enumerate(places)
    ]
    for load in tile_loads[:1]:
        load.start()
    weight_load = pltpu.make_async_copy(weight_hbm, weight_ref, load_sems.at[7])

    barrier = pltpu.get_barrier_semaphore()
    everyone = dev_a + dev_b + dev_z + [dev_b_far, dev_z_far, mate] + dev_other
    for device in everyone:
        pl.semaphore_signal(barrier, inc=1, device_id=device, device_id_type=MESH)

    sums[SLOTS] = jnp.zeros((BLOCK, BLOCK), jnp.float32)
    for load in small:
        load.wait()
    for load in tile_loads[1:] + [weight_load]:
        load.start()
    slot_table(target_ref[...], source_ref[...], count_ref, table_ref)
    to_scalars = pltpu.make_async_copy(table_ref, table, load_sems.at[8])
    to_scalars.start()
    to_scalars.wait()
    for load in block_loads:
        load.wait()

    def compute(i):
        tile_loads[i].wait()
        ja, jb = places[i]
        p = number(ja, jb)

        def group(g, total):
            products = []
            for u in range(UNROLL):
                slot = g * UNROLL + u
                products.append(
                    jnp.dot(
                        tiles[i][table[p, ORDER + slot]],
                        blocks[table[p, SOURCE + slot]],
                        preferred_element_type=jnp.float32,
                    )
                )
            for u in range(UNROLL):
                slot = g * UNROLL + u
                total = total * table[p, KEEP + slot].astype(jnp.float32) + products[u]
                sums[slot] = total
            return total

        lax.fori_loop(0, SLOTS // UNROLL, group, jnp.zeros((BLOCK, BLOCK), jnp.float32))
        for t in range(TARGETS):
            value = sums[table[p, LAST + t]]
            if i < 12:
                part[ja, jb, t // 4, (t % 4) * BLOCK : (t % 4 + 1) * BLOCK] = value.astype(jnp.bfloat16)
            else:
                row32[jb, t // 4, (t % 4) * BLOCK : (t % 4 + 1) * BLOCK] = value

    n = len(CHUNKS)
    starts = [sum(CHUNKS[:c]) for c in range(n)]

    def rows(c):
        return pl.ds(starts[c], CHUNKS[c])

    def copy(kind, c, src, dst, device):
        return pltpu.make_async_remote_copy(
            src_ref=src,
            dst_ref=dst,
            send_sem=send_sems.at[kind, c],
            recv_sem=recv_sems.at[kind, c],
            device_id=device,
            device_id_type=MESH,
        )

    def far1(jb, d):
        return copy(F1 + d, jb, part.at[far_a, jb, d], got1.at[0, d, jb], dev_a[d])

    def first(kind, c, d):
        if kind == P1:
            src = part.at[near_a[d], :, 1 - d, rows(c)]
        else:
            src = mix1.at[d, :, rows(c)]
        return copy(kind + d, c, src, got1.at[kind // 2, d, :, rows(c)], dev_a[d])

    def second(kind, c, d):
        if kind == F2:
            src = row16.at[far_b, d, rows(c)]
        elif kind == P2:
            src = row16.at[near_b[d], 1 - d, rows(c)]
        else:
            src = mix2.at[d, rows(c)]
        return copy(kind + d, c, src, got2.at[(kind - F2) // 2, d, rows(c)], dev_b[d])

    def straight(c):
        return [
            copy(C2 + d, c, row16.at[near_b[d], :, rows(c)], gotd.at[d, :, rows(c)], dev_b[d]) for d in (0, 1)
        ] + [copy(F2, c, row16.at[far_b, :, rows(c)], gotd.at[2, :, rows(c)], dev_b_far)]

    def along_z(c):
        here = hidden.at[feat, :, rows(c)]
        return [copy(ZNEAR + d, c, here, here, dev_z[d]) for d in (0, 1)] + [copy(ZFAR, c, here, here, dev_z_far)]

    def to_mate(kind, c, chip):
        here = hidden.at[chip * 2 + core, :, rows(c)]
        return copy(kind, c, here, here, mate)

    def mate_copies(c):
        if c in BOTH:
            here = hidden.at[feat, :, rows(c)]
            return [to_mate(OWN, c, z)] + [
                copy(kind, c, here, here, device) for kind, device in zip((FWD0, FWD1, FWD2), dev_other)
            ]
        return [
            to_mate(OWN, c, z),
            to_mate(FWD0, c, near_z[0]),
            to_mate(FWD1, c, near_z[1]),
            to_mate(FWD2, c, far_z),
        ]

    def stage1(c):
        for d in (0, 1):
            for jb in range(RING):
                if c == 0:
                    far1(jb, d).wait_recv()

            def add(jb, carry):
                mix1[d, jb, rows(c)] = (
                    part[near_a[d], jb, d, rows(c)].astype(jnp.float32)
                    + got1[0, d, jb, rows(c)].astype(jnp.float32)
                ).astype(jnp.bfloat16)
                return carry

            lax.fori_loop(0, RING, add, 0)
            first(C1, c, d).start()
        if c + AHEAD < n:
            for d in (0, 1):
                first(P1, c + AHEAD, d).start()

    def stage2(c):
        for d in (0, 1):
            first(C1, c, d).wait_recv()
            first(P1, c, d).wait_recv()

        def add(jb, carry):
            for d in (0, 1):
                value = (
                    row32[jb, d, rows(c)]
                    + got1[1, d, jb, rows(c)].astype(jnp.float32)
                    + got1[2, 1 - d, jb, rows(c)].astype(jnp.float32)
                )
                row32[jb, d, rows(c)] = value
                row16[jb, d, rows(c)] = value.astype(jnp.bfloat16)
            return carry

        lax.fori_loop(0, RING, add, 0)
        if c in DIRECT:
            for s in straight(c):
                s.start()
        else:
            for d in (0, 1):
                second(F2, c, d).start()
            for d in (0, 1):
                second(P2, c, d).start()

    def stage3(c):
        if c in DIRECT:
            return
        for d in (0, 1):
            second(F2, c, d).wait_recv()
            mix2[d, rows(c)] = (
                row32[near_b[d], d, rows(c)] + got2[0, d, rows(c)].astype(jnp.float32)
            ).astype(jnp.bfloat16)
            second(C2, c, d).start()

    def stage4(c):
        if c in DIRECT:
            for s in straight(c):
                s.wait_recv()
            for d in (0, 1):
                hidden[feat, d, rows(c)] = (
                    row32[ib, d, rows(c)]
                    + gotd[0, d, rows(c)].astype(jnp.float32)
                    + gotd[1, d, rows(c)].astype(jnp.float32)
                    + gotd[2, d, rows(c)].astype(jnp.float32)
                ).astype(jnp.bfloat16)
        else:
            for d in (0, 1):
                second(C2, c, d).wait_recv()
                second(P2, c, d).wait_recv()
            for d in (0, 1):
                hidden[feat, d, rows(c)] = (
                    row32[ib, d, rows(c)]
                    + got2[1, d, rows(c)].astype(jnp.float32)
                    + got2[2, 1 - d, rows(c)].astype(jnp.float32)
                ).astype(jnp.bfloat16)
        for s in along_z(c):
            s.start()
        for s in mate_copies(c) if c in BOTH else [to_mate(OWN, c, z)]:
            s.start()

    def stage5(c):
        for s, kind, chip in zip(along_z(c), (FWD1, FWD0, FWD2), (near_z[1], near_z[0], far_z)):
            s.wait_recv()
            if c not in BOTH:
                to_mate(kind, c, chip).start()

    def stage6(c):
        if c == 0:
            weight_load.wait()
        for m in mate_copies(c):
            m.wait_recv()
        total = jnp.zeros((2 * CHUNKS[c], BLOCK), jnp.float32)
        for f in range(2 * RING):
            total += jnp.dot(
                hidden[f, :, rows(c)].reshape(2 * CHUNKS[c], BLOCK),
                weight_ref[f * BLOCK : (f + 1) * BLOCK, :],
                preferred_element_type=jnp.float32,
            )
        value = jnp.maximum(total, 0.0).astype(out_ref.dtype)
        for d in (0, 1):
            out_ref[d, rows(c)] = value[d * CHUNKS[c] : (d + 1) * CHUNKS[c]]

    for i in range(PIECES):
        compute(i)
        if i == 0:
            pl.semaphore_wait(barrier, len(everyone))
        if i < RING:
            for d in (0, 1):
                far1(i, d).start()
        if i in (2 * RING - 1, 3 * RING - 1):
            for c in range(AHEAD):
                first(P1, c, i // RING - 1).start()
    stages = (stage1, stage2, stage3, stage4, stage5, stage6)
    for t in range(n + LAGS[-1]):
        for lag, stage in zip(LAGS, stages):
            if 0 <= t - lag < n:
                stage(t - lag)

    for d in (0, 1):
        for jb in range(RING):
            far1(jb, d).wait_send()
    for c in range(n):
        for d in (0, 1):
            for kind in (C1, P1):
                first(kind, c, d).wait_send()
        if c in DIRECT:
            for s in straight(c):
                s.wait_send()
        else:
            for d in (0, 1):
                for kind in (F2, C2, P2):
                    second(kind, c, d).wait_send()
        for s in along_z(c) + mate_copies(c):
            s.wait_send()


def layer(target, source, count, adj, blocks, weight):
    half = TGT_DEV // 2
    n = len(CHUNKS)
    hbm = pl.BlockSpec(memory_space=pltpu.HBM)
    bf16, f32 = jnp.bfloat16, jnp.float32
    return pl.pallas_call(
        layer_kernel,
        out_shape=pltpu.VMEM((2, half, BLOCK), bf16),
        in_specs=[hbm] * 6,
        out_specs=pl.BlockSpec(memory_space=pltpu.VMEM),
        scratch_shapes=[
            pltpu.VMEM(target.shape, jnp.int32),
            pltpu.VMEM(source.shape, jnp.int32),
            pltpu.SMEM(count.shape, jnp.int32),
            pltpu.VMEM((PIECES, 4 * SLOTS), jnp.int32),
            pltpu.SMEM((PIECES, 4 * SLOTS), jnp.int32),
            pltpu.VMEM(blocks.shape, bf16),
            pltpu.VMEM(weight.shape, bf16),
            pltpu.VMEM((SLOTS + 1, BLOCK, BLOCK), f32),
            pltpu.VMEM((RING, RING, 2, half, BLOCK), bf16),
            pltpu.VMEM((3, 2, RING, half, BLOCK), bf16),
            pltpu.VMEM((2, RING, half, BLOCK), bf16),
            pltpu.VMEM((RING, 2, half, BLOCK), f32),
            pltpu.VMEM((RING, 2, half, BLOCK), bf16),
            pltpu.VMEM((3, 2, half, BLOCK), bf16),
            pltpu.VMEM((2, half, BLOCK), bf16),
            pltpu.VMEM((3, 2, half, BLOCK), bf16),
            pltpu.VMEM((2 * RING, 2, half, BLOCK), bf16),
            pltpu.SemaphoreType.DMA((9,)),
            pltpu.SemaphoreType.DMA((PIECES,)),
            pltpu.SemaphoreType.DMA((KINDS, n)),
            pltpu.SemaphoreType.DMA((KINDS, n)),
        ]
        + [pltpu.VMEM(adj.shape[1:], bf16) for _ in range(PIECES)],
        compiler_params=pltpu.CompilerParams(
            collective_id=0, has_side_effects=True, vmem_limit_bytes=VMEM_LIMIT
        ),
        name="layer",
    )(target, source, count, adj, blocks, weight).reshape(TGT_DEV, BLOCK)


def body(sources, adjacency, target_block, source_block, slot_counts, weight):
    blocks = sources.reshape(sources.shape[0] // BLOCK, BLOCK, sources.shape[1])
    return layer(target_block[0], source_block[0], slot_counts, adjacency[0], blocks, weight)


def solution(mesh):
    return jax.shard_map(
        body,
        mesh=mesh,
        in_specs=(
            P(("blk", "sub"), "feat"),
            P(("blk", "sub"), None, None, None, None),
            P(("blk", "sub"), None, None),
            P(("blk", "sub"), None, None),
            P(("blk", "sub"), None),
            P(None, "feat"),
        ),
        out_specs=P(("blk", "sub"), "feat"),
        check_vma=False,
    )
```

```python
import jax
import jax.numpy as jnp
from jax import lax
from jax.experimental import pallas as pl
from jax.experimental.pallas import tpu as pltpu
from jax.sharding import PartitionSpec as P

BLOCK = 128
TGT_DEV = 1024
SLOTS = 32
RING = 4
PIECES = RING * RING
TARGETS = TGT_DEV // BLOCK
UNROLL = 32
CHUNKS = (160, 160, 128, 64)
DIRECT = (0, 1, 2, 3)
AHEAD = 2
BOTH = (3,)
VMEM_LIMIT = 56 << 20
STEPS = ((2, 0), (2, 1), (4, 0), (2, 2), (4, 1), (2, 3), (5, 0), (4, 2), (6, 0), (5, 1), (4, 3), (6, 1), (5, 2), (6, 2), (5, 3), (6, 3))
MESH = pl.DeviceIdType.MESH

F1, C1, P1, F2, C2, P2, ZNEAR = range(0, 14, 2)
ZFAR, OWN, FWD0, FWD1, FWD2 = range(14, 19)
KINDS = 19

ORDER, SOURCE, KEEP, LAST = 0, SLOTS, 2 * SLOTS, 3 * SLOTS


def slot_table(target, source, count_ref, table):
    shape = target.shape
    row = lax.broadcasted_iota(jnp.int32, shape, 0)
    lane = lax.broadcasted_iota(jnp.int32, shape, 1)
    count = jnp.zeros(shape, jnp.int32)
    for p in range(PIECES):
        count = jnp.where(row == p, count_ref[0, p], count)
    key = jnp.where(lane < count, target, TARGETS)
    unique = key * SLOTS + lane
    rank = jnp.zeros(shape, jnp.int32)
    earlier = jnp.zeros(shape, jnp.int32)
    upto = jnp.zeros(shape, jnp.int32)
    hit = jnp.zeros(shape, jnp.int32)
    for j in range(SLOTS):
        key_j = jnp.broadcast_to(key[:, j : j + 1], shape)
        rank += jnp.where(key_j * SLOTS + j < unique, 1, 0)
        earlier += jnp.where((key_j == key) & (lane > j), 1, 0)
        upto += jnp.where(key_j <= lane, 1, 0)
        hit += jnp.where(key_j == lane, 1, 0)
    keep = jnp.where(earlier > 0, 1, 0)
    order = jnp.zeros(shape, jnp.int32)
    source_of = jnp.zeros(shape, jnp.int32)
    keep_of = jnp.zeros(shape, jnp.int32)
    for k in range(SLOTS):
        here = jnp.broadcast_to(rank[:, k : k + 1], shape) == lane
        order = jnp.where(here, k, order)
        source_of = jnp.where(here, jnp.broadcast_to(source[:, k : k + 1], shape), source_of)
        keep_of = jnp.where(here, jnp.broadcast_to(keep[:, k : k + 1], shape), keep_of)
    table[:, ORDER : ORDER + SLOTS] = order
    table[:, SOURCE : SOURCE + SLOTS] = source_of
    table[:, KEEP : KEEP + SLOTS] = keep_of
    table[:, LAST : LAST + SLOTS] = jnp.where(hit > 0, upto - 1, SLOTS)


def layer_kernel(
    target_hbm, source_hbm, count_hbm, adj_hbm, blocks_hbm, weight_hbm, out_ref, *scratch
):
    (target_ref, source_ref, count_ref, table_ref, table, blocks, weight_ref, sums, part, got1, mix1,
     row32, row16, got2, mix2, gotd, hidden, load_sems, adj_sems, send_sems, recv_sems) = scratch[:21]
    tiles = scratch[21:]

    blk, sub, feat = lax.axis_index("blk"), lax.axis_index("sub"), lax.axis_index("feat")
    x, y = blk // 2, (blk % 2) * 2 + sub
    z, core = feat // 2, feat % 2
    ia = x * (1 - core) + y * core
    ib = y * (1 - core) + x * core

    def at(ja, jb, jz, jcore):
        px = ja * (1 - core) + jb * core
        py = jb * (1 - core) + ja * core
        return (px * 2 + py // 2, py % 2, jz * 2 + jcore)

    step = (1, RING - 1)
    near_a = [(ia + s) % RING for s in step]
    near_b = [(ib + s) % RING for s in step]
    near_z = [(z + s) % RING for s in step]
    far_a, far_b, far_z = (ia + 2) % RING, (ib + 2) % RING, (z + 2) % RING
    dev_a = [at(j, ib, z, core) for j in near_a]
    dev_b = [at(ia, j, z, core) for j in near_b]
    dev_z = [at(ia, ib, j, core) for j in near_z]
    dev_b_far = at(ia, far_b, z, core)
    dev_z_far = at(ia, ib, far_z, core)
    dev_other = [at(ia, ib, j, 1 - core) for j in (near_z[0], near_z[1], far_z)]
    mate = (blk, sub, z * 2 + 1 - core)

    small = [
        pltpu.make_async_copy(target_hbm, target_ref, load_sems.at[0]),
        pltpu.make_async_copy(source_hbm, source_ref, load_sems.at[1]),
        pltpu.make_async_copy(count_hbm, count_ref, load_sems.at[2]),
    ]
    for load in small:
        load.start()
    quarter = blocks.shape[0] // 4
    block_loads = [
        pltpu.make_async_copy(
            blocks_hbm.at[pl.ds(q * quarter, quarter)], blocks.at[pl.ds(q * quarter, quarter)], load_sems.at[3 + q]
        )
        for q in range(4)
    ]
    for load in block_loads:
        load.start()
    places = [(ja, jb) for ja in (far_a, near_a[0], near_a[1], ia) for jb in (0, 1, 2, 3)]

    def number(ja, jb):
        return (ja * (1 - core) + jb * core) * RING + jb * (1 - core) + ja * core

    tile_loads = [
        pltpu.make_async_copy(adj_hbm.at[number(ja, jb)], tiles[i], adj_sems.at[i])
        for i, (ja, jb) in enumerate(places)
    ]
    for load in tile_loads[:1]:
        load.start()
    weight_load = pltpu.make_async_copy(weight_hbm, weight_ref, load_sems.at[7])

    barrier = pltpu.get_barrier_semaphore()
    everyone = dev_a + dev_b + dev_z + [dev_b_far, dev_z_far, mate] + dev_other
    for device in everyone:
        pl.semaphore_signal(barrier, inc=1, device_id=device, device_id_type=MESH)

    sums[SLOTS] = jnp.zeros((BLOCK, BLOCK), jnp.float32)
    for load in small:
        load.wait()
    for load in tile_loads[1:] + [weight_load]:
        load.start()
    slot_table(target_ref[...], source_ref[...], count_ref, table_ref)
    to_scalars = pltpu.make_async_copy(table_ref, table, load_sems.at[8])
    to_scalars.start()
    to_scalars.wait()
    for load in block_loads:
        load.wait()

    def compute(i):
        tile_loads[i].wait()
        ja, jb = places[i]
        p = number(ja, jb)

        def group(g, total):
            products = []
            for u in range(UNROLL):
                slot = g * UNROLL + u
                products.append(
                    jnp.dot(
                        tiles[i][table[p, ORDER + slot]],
                        blocks[table[p, SOURCE + slot]],
                        preferred_element_type=jnp.float32,
                    )
                )
            for u in range(UNROLL):
                slot = g * UNROLL + u
                total = total * table[p, KEEP + slot].astype(jnp.float32) + products[u]
                sums[slot] = total
            return total

        lax.fori_loop(0, SLOTS // UNROLL, group, jnp.zeros((BLOCK, BLOCK), jnp.float32))
        for t in range(TARGETS):
            value = sums[table[p, LAST + t]]
            if i < 12:
                part[ja, jb, t // 4, (t % 4) * BLOCK : (t % 4 + 1) * BLOCK] = value.astype(jnp.bfloat16)
            else:
                row32[jb, t // 4, (t % 4) * BLOCK : (t % 4 + 1) * BLOCK] = value

    n = len(CHUNKS)
    starts = [sum(CHUNKS[:c]) for c in range(n)]

    def rows(c):
        return pl.ds(starts[c], CHUNKS[c])

    def copy(kind, c, src, dst, device):
        return pltpu.make_async_remote_copy(
            src_ref=src,
            dst_ref=dst,
            send_sem=send_sems.at[kind, c],
            recv_sem=recv_sems.at[kind, c],
            device_id=device,
            device_id_type=MESH,
        )

    def far1(jb, d):
        return copy(F1 + d, jb, part.at[far_a, jb, d], got1.at[0, d, jb], dev_a[d])

    def first(kind, c, d):
        if kind == P1:
            src = part.at[near_a[d], :, 1 - d, rows(c)]
        else:
            src = mix1.at[d, :, rows(c)]
        return copy(kind + d, c, src, got1.at[kind // 2, d, :, rows(c)], dev_a[d])

    def second(kind, c, d):
        if kind == F2:
            src = row16.at[far_b, d, rows(c)]
        elif kind == P2:
            src = row16.at[near_b[d], 1 - d, rows(c)]
        else:
            src = mix2.at[d, rows(c)]
        return copy(kind + d, c, src, got2.at[(kind - F2) // 2, d, rows(c)], dev_b[d])

    def straight(c):
        return [
            copy(C2 + d, c, row16.at[near_b[d], :, rows(c)], gotd.at[d, :, rows(c)], dev_b[d]) for d in (0, 1)
        ] + [copy(F2, c, row16.at[far_b, :, rows(c)], gotd.at[2, :, rows(c)], dev_b_far)]

    def along_z(c):
        here = hidden.at[feat, :, rows(c)]
        return [copy(ZNEAR + d, c, here, here, dev_z[d]) for d in (0, 1)] + [copy(ZFAR, c, here, here, dev_z_far)]

    def to_mate(kind, c, chip):
        here = hidden.at[chip * 2 + core, :, rows(c)]
        return copy(kind, c, here, here, mate)

    def mate_copies(c):
        if c in BOTH:
            here = hidden.at[feat, :, rows(c)]
            return [to_mate(OWN, c, z)] + [
                copy(kind, c, here, here, device) for kind, device in zip((FWD0, FWD1, FWD2), dev_other)
            ]
        return [
            to_mate(OWN, c, z),
            to_mate(FWD0, c, near_z[0]),
            to_mate(FWD1, c, near_z[1]),
            to_mate(FWD2, c, far_z),
        ]

    def stage1(c):
        for d in (0, 1):
            for jb in range(RING):
                if c == 0:
                    far1(jb, d).wait_recv()

            def add(jb, carry):
                mix1[d, jb, rows(c)] = (
                    part[near_a[d], jb, d, rows(c)].astype(jnp.float32)
                    + got1[0, d, jb, rows(c)].astype(jnp.float32)
                ).astype(jnp.bfloat16)
                return carry

            lax.fori_loop(0, RING, add, 0)
            first(C1, c, d).start()
        if c + AHEAD < n:
            for d in (0, 1):
                first(P1, c + AHEAD, d).start()

    def stage2(c):
        for d in (0, 1):
            first(C1, c, d).wait_recv()
            first(P1, c, d).wait_recv()

        def add(jb, carry):
            for d in (0, 1):
                value = (
                    row32[jb, d, rows(c)]
                    + got1[1, d, jb, rows(c)].astype(jnp.float32)
                    + got1[2, 1 - d, jb, rows(c)].astype(jnp.float32)
                )
                row32[jb, d, rows(c)] = value
                row16[jb, d, rows(c)] = value.astype(jnp.bfloat16)
            return carry

        lax.fori_loop(0, RING, add, 0)
        if c in DIRECT:
            for s in straight(c):
                s.start()
        else:
            for d in (0, 1):
                second(F2, c, d).start()
            for d in (0, 1):
                second(P2, c, d).start()

    def stage3(c):
        if c in DIRECT:
            return
        for d in (0, 1):
            second(F2, c, d).wait_recv()
            mix2[d, rows(c)] = (
                row32[near_b[d], d, rows(c)] + got2[0, d, rows(c)].astype(jnp.float32)
            ).astype(jnp.bfloat16)
            second(C2, c, d).start()

    def stage4(c):
        if c in DIRECT:
            for s in straight(c):
                s.wait_recv()
            for d in (0, 1):
                hidden[feat, d, rows(c)] = (
                    row32[ib, d, rows(c)]
                    + gotd[0, d, rows(c)].astype(jnp.float32)
                    + gotd[1, d, rows(c)].astype(jnp.float32)
                    + gotd[2, d, rows(c)].astype(jnp.float32)
                ).astype(jnp.bfloat16)
        else:
            for d in (0, 1):
                second(C2, c, d).wait_recv()
                second(P2, c, d).wait_recv()
            for d in (0, 1):
                hidden[feat, d, rows(c)] = (
                    row32[ib, d, rows(c)]
                    + got2[1, d, rows(c)].astype(jnp.float32)
                    + got2[2, 1 - d, rows(c)].astype(jnp.float32)
                ).astype(jnp.bfloat16)
        for s in along_z(c):
            s.start()
        for s in mate_copies(c) if c in BOTH else [to_mate(OWN, c, z)]:
            s.start()

    def stage5(c):
        for s, kind, chip in zip(along_z(c), (FWD1, FWD0, FWD2), (near_z[1], near_z[0], far_z)):
            s.wait_recv()
            if c not in BOTH:
                to_mate(kind, c, chip).start()

    def stage6(c):
        if c == 0:
            weight_load.wait()
        for m in mate_copies(c):
            m.wait_recv()
        total = jnp.zeros((2 * CHUNKS[c], BLOCK), jnp.float32)
        for f in range(2 * RING):
            total += jnp.dot(
                hidden[f, :, rows(c)].reshape(2 * CHUNKS[c], BLOCK),
                weight_ref[f * BLOCK : (f + 1) * BLOCK, :],
                preferred_element_type=jnp.float32,
            )
        value = jnp.maximum(total, 0.0).astype(out_ref.dtype)
        for d in (0, 1):
            out_ref[d, rows(c)] = value[d * CHUNKS[c] : (d + 1) * CHUNKS[c]]

    for i in range(PIECES):
        compute(i)
        if i == 0:
            pl.semaphore_wait(barrier, len(everyone))
        if i < RING:
            for d in (0, 1):
                far1(i, d).start()
        if i in (2 * RING - 1, 3 * RING - 1):
            for c in range(AHEAD):
                first(P1, c, i // RING - 1).start()
    for c in range(n):
        stage1(c)
    stages = {2: stage2, 4: stage4, 5: stage5, 6: stage6}
    for stage, c in STEPS:
        stages[stage](c)

    for d in (0, 1):
        for jb in range(RING):
            far1(jb, d).wait_send()
    for c in range(n):
        for d in (0, 1):
            for kind in (C1, P1):
                first(kind, c, d).wait_send()
        if c in DIRECT:
            for s in straight(c):
                s.wait_send()
        else:
            for d in (0, 1):
                for kind in (F2, C2, P2):
                    second(kind, c, d).wait_send()
        for s in along_z(c) + mate_copies(c):
            s.wait_send()


def layer(target, source, count, adj, blocks, weight):
    half = TGT_DEV // 2
    n = len(CHUNKS)
    hbm = pl.BlockSpec(memory_space=pltpu.HBM)
    bf16, f32 = jnp.bfloat16, jnp.float32
    return pl.pallas_call(
        layer_kernel,
        out_shape=pltpu.VMEM((2, half, BLOCK), bf16),
        in_specs=[hbm] * 6,
        out_specs=pl.BlockSpec(memory_space=pltpu.VMEM),
        scratch_shapes=[
            pltpu.VMEM(target.shape, jnp.int32),
            pltpu.VMEM(source.shape, jnp.int32),
            pltpu.SMEM(count.shape, jnp.int32),
            pltpu.VMEM((PIECES, 4 * SLOTS), jnp.int32),
            pltpu.SMEM((PIECES, 4 * SLOTS), jnp.int32),
            pltpu.VMEM(blocks.shape, bf16),
            pltpu.VMEM(weight.shape, bf16),
            pltpu.VMEM((SLOTS + 1, BLOCK, BLOCK), f32),
            pltpu.VMEM((RING, RING, 2, half, BLOCK), bf16),
            pltpu.VMEM((3, 2, RING, half, BLOCK), bf16),
            pltpu.VMEM((2, RING, half, BLOCK), bf16),
            pltpu.VMEM((RING, 2, half, BLOCK), f32),
            pltpu.VMEM((RING, 2, half, BLOCK), bf16),
            pltpu.VMEM((3, 2, half, BLOCK), bf16),
            pltpu.VMEM((2, half, BLOCK), bf16),
            pltpu.VMEM((3, 2, half, BLOCK), bf16),
            pltpu.VMEM((2 * RING, 2, half, BLOCK), bf16),
            pltpu.SemaphoreType.DMA((9,)),
            pltpu.SemaphoreType.DMA((PIECES,)),
            pltpu.SemaphoreType.DMA((KINDS, n)),
            pltpu.SemaphoreType.DMA((KINDS, n)),
        ]
        + [pltpu.VMEM(adj.shape[1:], bf16) for _ in range(PIECES)],
        compiler_params=pltpu.CompilerParams(
            collective_id=0, has_side_effects=True, vmem_limit_bytes=VMEM_LIMIT
        ),
        name="layer",
    )(target, source, count, adj, blocks, weight).reshape(TGT_DEV, BLOCK)


def body(sources, adjacency, target_block, source_block, slot_counts, weight):
    blocks = sources.reshape(sources.shape[0] // BLOCK, BLOCK, sources.shape[1])
    return layer(target_block[0], source_block[0], slot_counts, adjacency[0], blocks, weight)


def solution(mesh):
    return jax.shard_map(
        body,
        mesh=mesh,
        in_specs=(
            P(("blk", "sub"), "feat"),
            P(("blk", "sub"), None, None, None, None),
            P(("blk", "sub"), None, None),
            P(("blk", "sub"), None, None),
            P(("blk", "sub"), None),
            P(None, "feat"),
        ),
        out_specs=P(("blk", "sub"), "feat"),
        check_vma=False,
    )
```
